512 devices in a mesh: ad: 64 (over z, x), tp: 8 (over y, core).
Axes of the slice: x: 4, y: 4, z: 16, core: 2. Of those that a mesh axis runs over, the one named last changes fastest.
Arguments:
- tokens: bfloat16 [4, 3072, 8192], P(None, 'ad', 'tp'), may hold values from -6 to 6
- row_adapter_index: int32 [4, 3072], P(None, 'ad'), may hold values from 0 to 255, as said below
- key_base_weight: bfloat16 [8192, 1024], P('tp'), may hold values from -0.0625 to 0.0625
- adapter_down_weight: bfloat16 [256, 8192, 64], P('ad', 'tp'), may hold values from -0.0625 to 0.0625
- adapter_up_weight: bfloat16 [256, 64, 1024], P('ad', None, 'tp'), may hold values from -0.75 to 0.75
Outputs:
- token_keys_output: bfloat16 [4, 3072, 1024], P(None, 'ad', 'tp')
The draws below stay inside these ranges and needn't reach their ends.
Inputs may be any that keep to these rules, and one draw needn't show every extreme that they name: `row_adapter_index`: group g holds adapters g * 4 to (g + 1) * 4 - 1. In each step the 48 rows of one index of ad name one group in exactly 2 rows and every other group in at most 1 row; that busiest group is the same for every index of ad in a step, so it receives 2 rows from each.
All inputs are finite; a program needn't handle non-finite values.
Results may differ from the reference program's by a relative error of at most 0.005.
Values may be sent and summed in bfloat16 or wider, within the bound.
A program may use at most 64 MiB of HBM per device.

```python
import jax
import jax.numpy as jnp
from jax import lax

MODEL_WIDTH = 8192
KEY_WIDTH = 1024
ADAPTER_RANK = 64
AD_DEV = 4
DECODE_STEPS = 4
ROW_DEV = 48
TOKEN_ROWS = 3072
ADAPTER_TOTAL = 256
CAP = 2


def draw_row_adapter_index(key, part):
    groups = TOKEN_ROWS // ROW_DEV
    key_busy, key_offsets, key_shuffle, key_local = jax.random.split(key, 4)
    busiest = jax.random.randint(key_busy, (DECODE_STEPS, 1, 1), 0, groups)
    offsets = jax.random.randint(key_offsets, (DECODE_STEPS, groups, 1), 0, groups - 1)
    position = jnp.arange(ROW_DEV, dtype=jnp.int32)[None, None, :]
    others = (busiest + 1 + (position - CAP + offsets) % (groups - 1)) % groups
    owner_group = jnp.where(position < CAP, busiest, others) * jnp.ones((DECODE_STEPS, groups, ROW_DEV), jnp.int32)
    subkeys = jax.random.split(key_shuffle, DECODE_STEPS * groups)
    shuffle_order = jax.vmap(lambda subkey: jax.random.permutation(subkey, ROW_DEV))(subkeys)
    shuffle_order = shuffle_order.reshape(DECODE_STEPS, groups, ROW_DEV).astype(jnp.int32)
    owner_group = jnp.take_along_axis(owner_group, shuffle_order, axis=2)
    local_index = jax.random.randint(key_local, (DECODE_STEPS, groups, ROW_DEV), 0, AD_DEV)
    return (owner_group * AD_DEV + local_index).reshape(DECODE_STEPS, TOKEN_ROWS).astype(jnp.int32)


def levels(key, dims, pieces, smallest, largest):
    def one(dim, parts):
        steps = jax.random.uniform(jax.random.fold_in(jax.random.fold_in(key, 6), dim), (parts,), jnp.float32, smallest / len(pieces), largest / len(pieces))
        return jnp.repeat(jnp.exp(steps), dims[dim] // parts).reshape((-1,) + (1,) * (len(dims) - dim - 1))

    gain = one(*pieces[0])
    for cut in pieces[1:]:
        gain = gain * one(*cut)
    return gain


def normal_values(stream_key, dims, spread, most, cuts=(), kind=jnp.bfloat16):
    loudness = levels(stream_key, dims, cuts, -0.22, 0.18) if cuts else 1.0
    drawn = jax.random.normal(stream_key, dims, jnp.float32) * spread * loudness
    return jnp.minimum(jnp.maximum(drawn, -most), most).astype(kind)


def setup_inputs(seed: int = 0) -> dict:
    seeds = jax.random.split(jax.random.key(seed), 6)
    return {
        "tokens": normal_values(seeds[0], (DECODE_STEPS, TOKEN_ROWS, MODEL_WIDTH), 1.0, 6.0, ((1, 64), (2, 8))),
        "row_adapter_index": draw_row_adapter_index(jax.random.fold_in(seeds[5], 71), 0),
        "key_base_weight": normal_values(seeds[2], (MODEL_WIDTH, KEY_WIDTH), MODEL_WIDTH ** -0.5, 0.0625, ((0, 8),)),
        "adapter_down_weight": normal_values(seeds[3], (ADAPTER_TOTAL, MODEL_WIDTH, ADAPTER_RANK), MODEL_WIDTH ** -0.5, 0.0625, ((0, 64), (1, 8))),
        "adapter_up_weight": normal_values(seeds[4], (ADAPTER_TOTAL, ADAPTER_RANK, KEY_WIDTH), ADAPTER_RANK ** -0.5, 0.75, ((0, 64), (2, 8))),
    }


def reference(tokens, row_adapter_index, key_base_weight, adapter_down_weight, adapter_up_weight):
    gathered_rows = tokens.reshape(DECODE_STEPS * TOKEN_ROWS, MODEL_WIDTH)
    base_keys_output = jnp.dot(gathered_rows, key_base_weight, preferred_element_type=jnp.float32)
    row_index_list = row_adapter_index.reshape(DECODE_STEPS * TOKEN_ROWS // 64, 64).astype(jnp.int32)

    def apply_row_block(args):
        block_rows, block_index_list = args
        down_weight_tiles = jnp.take(adapter_down_weight, block_index_list, axis=0).astype(jnp.float32)
        down_sum = jnp.einsum('nd,ndr->nr', block_rows.astype(jnp.float32), down_weight_tiles)
        down_low = lax.optimization_barrier(down_sum.astype(jnp.bfloat16)).astype(jnp.float32)
        up_weight_tiles = jnp.take(adapter_up_weight, block_index_list, axis=0).astype(jnp.float32)
        return jnp.einsum('nr,nrk->nk', down_low, up_weight_tiles).astype(jnp.bfloat16)

    adapter_update = lax.map(apply_row_block, (gathered_rows.reshape(DECODE_STEPS * TOKEN_ROWS // 64, 64, MODEL_WIDTH), row_index_list))
    adapter_update = adapter_update.reshape(DECODE_STEPS * TOKEN_ROWS, KEY_WIDTH)
    token_keys_output = (base_keys_output + adapter_update.astype(jnp.float32)).astype(jnp.bfloat16)
    return token_keys_output.reshape(DECODE_STEPS, TOKEN_ROWS, KEY_WIDTH)
```

```python
import jax
import jax.numpy as jnp
from jax import lax
from jax.sharding import PartitionSpec as P

CAP = 2
TAG_WIDTH = 128


def body(tokens, row_adapter_index, key_base_weight, adapter_down_weight, adapter_up_weight):
    step_count, row_dev, width_per_shard = tokens.shape
    groups = lax.axis_size("ad")
    adapter_number = adapter_down_weight.shape[0]
    rank = adapter_down_weight.shape[2]
    row_total = step_count * row_dev
    slots_per_group = step_count * CAP
    slot_total = groups * slots_per_group

    gathered_rows = tokens.reshape(row_total, width_per_shard)
    partial_base = jnp.dot(gathered_rows, key_base_weight, preferred_element_type=jnp.float32)
    base_keys_output = lax.psum_scatter(partial_base, "tp", scatter_dimension=1, tiled=True)
    key_feature_width = base_keys_output.shape[1]

    index_list = row_adapter_index.reshape(step_count, row_dev)
    owner_group = index_list // adapter_number
    local_index = index_list % adapter_number
    group_hits = (owner_group[:, :, None] == jnp.arange(groups, dtype=jnp.int32)[None, None, :]).astype(
        jnp.int32
    )
    slot_rank = jnp.sum((jnp.cumsum(group_hits, axis=1) - group_hits) * group_hits, axis=2)
    step_ids = jnp.arange(step_count, dtype=jnp.int32)[:, None]
    slot_index = (owner_group * slots_per_group + step_ids * CAP + slot_rank).reshape(row_total)
    dispatch = (
        slot_index[None, :] == jnp.arange(slot_total, dtype=jnp.int32)[:, None]
    ).astype(jnp.bfloat16)

    tag_values = (local_index + 1).astype(jnp.bfloat16).reshape(row_total, 1)
    tag_block = jnp.broadcast_to(tag_values, (row_total, TAG_WIDTH))
    rows_tagged = jnp.concatenate([gathered_rows, tag_block], axis=1)
    send_rows = jnp.dot(dispatch, rows_tagged, preferred_element_type=jnp.float32).astype(jnp.bfloat16)
    send_rows = send_rows.reshape(groups, slots_per_group, width_per_shard + TAG_WIDTH)
    incoming = lax.all_to_all(send_rows, "ad", split_axis=0, concat_axis=0, tiled=True)
    incoming = incoming.reshape(slot_total, width_per_shard + TAG_WIDTH)
    incoming_rows = incoming[:, :width_per_shard]
    incoming_labels = incoming[:, width_per_shard]

    down_all = jnp.einsum(
        "nd,adr->nar", incoming_rows, adapter_down_weight, preferred_element_type=jnp.float32
    )
    labels = (jnp.arange(adapter_number, dtype=jnp.int32) + 1).astype(jnp.bfloat16)
    selector = (incoming_labels[:, None] == labels[None, :]).astype(jnp.float32)
    down_part = jnp.sum(down_all * selector[:, :, None], axis=1)
    down_sum = lax.psum(down_part, "tp")
    down_low = down_sum.astype(jnp.bfloat16)
    spread_rows = (selector.astype(jnp.bfloat16)[:, :, None] * down_low[:, None, :]).reshape(
        slot_total, adapter_number * rank
    )
    up_flat = adapter_up_weight.reshape(adapter_number * rank, key_feature_width)
    adapter_update = jnp.dot(spread_rows, up_flat, preferred_element_type=jnp.float32).astype(
        jnp.bfloat16
    )
    adapter_update = adapter_update.reshape(groups, slots_per_group, key_feature_width)
    rows_sent_back = lax.all_to_all(adapter_update, "ad", split_axis=0, concat_axis=0, tiled=True)
    routed = jnp.dot(
        dispatch.T,
        rows_sent_back.reshape(slot_total, key_feature_width),
        preferred_element_type=jnp.float32,
    )
    out = (base_keys_output + routed).astype(jnp.bfloat16)
    return out.reshape(step_count, row_dev, key_feature_width)


def solution(mesh):
    placed = (
        P(None, "ad", "tp"),
        P(None, "ad"),
        P("tp", None),
        P("ad", "tp", None),
        P("ad", None, "tp"),
    )
    return jax.shard_map(
        body, mesh=mesh, in_specs=placed, out_specs=P(None, "ad", "tp"), check_vma=False
    )
```

```python
import jax
import jax.numpy as jnp
from jax import lax
from jax.sharding import PartitionSpec as P

TAG_WIDTH = 128


def body(tokens, row_adapter_index, key_base_weight, adapter_down_weight, adapter_up_weight):
    step_count, row_dev, width_per_shard = tokens.shape
    groups = lax.axis_size("ad")
    me = lax.axis_index("ad")
    adapter_number = adapter_down_weight.shape[0]
    rank = adapter_down_weight.shape[2]
    row_total = step_count * row_dev
    regular_total = groups * step_count
    wide = width_per_shard + TAG_WIDTH

    gathered_rows = tokens.reshape(row_total, width_per_shard)

    index_list = row_adapter_index.reshape(step_count, row_dev)
    owner_group = index_list // adapter_number
    local_index = index_list % adapter_number
    group_hits = (owner_group[:, :, None] == jnp.arange(groups, dtype=jnp.int32)[None, None, :]).astype(
        jnp.int32
    )
    slot_rank = jnp.sum((jnp.cumsum(group_hits, axis=1) - group_hits) * group_hits, axis=2)
    step_ids = jnp.arange(step_count, dtype=jnp.int32)[:, None]
    first = slot_rank == 0
    regular_slot = jnp.where(first, owner_group * step_count + step_ids, -1).reshape(row_total)
    overflow_slot = jnp.where(slot_rank == 1, step_ids, -1).reshape(row_total)
    dispatch = (
        regular_slot[None, :] == jnp.arange(regular_total, dtype=jnp.int32)[:, None]
    ).astype(jnp.bfloat16)
    dispatch_over = (
        overflow_slot[None, :] == jnp.arange(step_count, dtype=jnp.int32)[:, None]
    ).astype(jnp.bfloat16)

    tag_values = jnp.where(first, local_index + 1, index_list + 1).astype(jnp.bfloat16)
    tag_block = jnp.broadcast_to(tag_values.reshape(row_total, 1), (row_total, TAG_WIDTH))
    rows_tagged = jnp.concatenate([gathered_rows, tag_block], axis=1)
    send_rows = jnp.dot(dispatch, rows_tagged, preferred_element_type=jnp.float32).astype(jnp.bfloat16)
    send_rows = send_rows.reshape(groups, step_count, wide)
    send_over = jnp.dot(dispatch_over, rows_tagged, preferred_element_type=jnp.float32).astype(
        jnp.bfloat16
    )
    incoming_over = lax.all_gather(send_over, "ad", tiled=True)
    incoming = lax.all_to_all(send_rows, "ad", split_axis=0, concat_axis=0, tiled=True)

    partial_base = jnp.dot(gathered_rows, key_base_weight, preferred_element_type=jnp.float32)
    partial_base, incoming_over = lax.optimization_barrier((partial_base, incoming_over))
    base_keys_output = lax.psum_scatter(partial_base, "tp", scatter_dimension=1, tiled=True)
    key_feature_width = base_keys_output.shape[1]

    incoming = jnp.concatenate([incoming.reshape(regular_total, wide), incoming_over], axis=0)
    slot_total = incoming.shape[0]
    incoming_rows = incoming[:, :width_per_shard]
    regular_labels = incoming[:regular_total, width_per_shard].astype(jnp.float32)
    over_labels = incoming[regular_total:, width_per_shard].astype(jnp.float32) - (
        me * adapter_number
    ).astype(jnp.float32)
    incoming_labels = jnp.concatenate([regular_labels, over_labels])

    down_all = jnp.einsum(
        "nd,adr->nar", incoming_rows, adapter_down_weight, preferred_element_type=jnp.float32
    )
    labels = (jnp.arange(adapter_number, dtype=jnp.int32) + 1).astype(jnp.float32)
    selector = (incoming_labels[:, None] == labels[None, :]).astype(jnp.float32)
    down_part = jnp.sum(down_all * selector[:, :, None], axis=1)
    down_sum = lax.psum(down_part, "tp")
    down_low = down_sum.astype(jnp.bfloat16)
    spread_rows = (selector.astype(jnp.bfloat16)[:, :, None] * down_low[:, None, :]).reshape(
        slot_total, adapter_number * rank
    )
    up_flat = adapter_up_weight.reshape(adapter_number * rank, key_feature_width)
    adapter_update = jnp.dot(spread_rows, up_flat, preferred_element_type=jnp.float32).astype(
        jnp.bfloat16
    )
    update_regular = adapter_update[:regular_total].reshape(groups, step_count, key_feature_width)
    update_over = adapter_update[regular_total:].reshape(groups, step_count, key_feature_width)
    send_back = jnp.concatenate([update_regular, update_over], axis=1)
    rows_sent_back = lax.all_to_all(send_back, "ad", split_axis=0, concat_axis=0, tiled=True)
    back_regular = rows_sent_back[:, :step_count].reshape(regular_total, key_feature_width)
    back_over = jnp.sum(rows_sent_back[:, step_count:].astype(jnp.float32), axis=0)
    routed = jnp.dot(dispatch.T, back_regular, preferred_element_type=jnp.float32) + jnp.dot(
        dispatch_over.T.astype(jnp.float32), back_over, preferred_element_type=jnp.float32
    )
    out = (base_keys_output + routed).astype(jnp.bfloat16)
    return out.reshape(step_count, row_dev, key_feature_width)


def solution(mesh):
    placed = (
        P(None, "ad", "tp"),
        P(None, "ad"),
        P("tp", None),
        P("ad", "tp", None),
        P("ad", None, "tp"),
    )
    return jax.shard_map(
        body, mesh=mesh, in_specs=placed, out_specs=P(None, "ad", "tp"), check_vma=False
    )
```

```python
import jax
import jax.numpy as jnp
from jax import lax
from jax.sharding import PartitionSpec as P

CAP = 2
TAG_WIDTH = 128


def body(tokens, row_adapter_index, key_base_weight, adapter_down_weight, adapter_up_weight):
    step_count, row_dev, width_per_shard = tokens.shape
    groups = lax.axis_size("ad")
    adapter_number = adapter_down_weight.shape[0]
    rank = adapter_down_weight.shape[2]
    row_total = step_count * row_dev
    slots_per_group = step_count * CAP
    slot_total = groups * slots_per_group

    gathered_rows = tokens.reshape(row_total, width_per_shard)
    partial_base = jnp.dot(gathered_rows, key_base_weight, preferred_element_type=jnp.float32)
    base_keys_output = lax.psum_scatter(partial_base, "tp", scatter_dimension=1, tiled=True)
    key_feature_width = base_keys_output.shape[1]

    index_list = row_adapter_index.reshape(step_count, row_dev)
    owner_group = index_list // adapter_number
    local_index = index_list % adapter_number
    group_hits = (owner_group[:, :, None] == jnp.arange(groups, dtype=jnp.int32)[None, None, :]).astype(
        jnp.int32
    )
    slot_rank = jnp.sum((jnp.cumsum(group_hits, axis=1) - group_hits) * group_hits, axis=2)
    step_ids = jnp.arange(step_count, dtype=jnp.int32)[:, None]
    slot_index = (owner_group * slots_per_group + step_ids * CAP + slot_rank).reshape(row_total)
    dispatch = (
        slot_index[None, :] == jnp.arange(slot_total, dtype=jnp.int32)[:, None]
    ).astype(jnp.bfloat16)

    tag_values = (local_index + 1).astype(jnp.bfloat16).reshape(row_total, 1)
    tag_block = jnp.broadcast_to(tag_values, (row_total, TAG_WIDTH))
    rows_tagged = jnp.concatenate([gathered_rows, tag_block], axis=1)
    send_rows = jnp.dot(dispatch, rows_tagged, preferred_element_type=jnp.float32).astype(jnp.bfloat16)
    send_rows = send_rows.reshape(groups, slots_per_group, width_per_shard + TAG_WIDTH)
    incoming = lax.all_to_all(send_rows, "ad", split_axis=0, concat_axis=0, tiled=True)
    incoming = incoming.reshape(slot_total, width_per_shard + TAG_WIDTH)
    incoming_rows = incoming[:, :width_per_shard]
    incoming_labels = incoming[:, width_per_shard]

    down_all = jnp.einsum(
        "nd,adr->nar", incoming_rows, adapter_down_weight, preferred_element_type=jnp.float32
    )
    labels = (jnp.arange(adapter_number, dtype=jnp.int32) + 1).astype(jnp.bfloat16)
    selector = (incoming_labels[:, None] == labels[None, :]).astype(jnp.float32)
    down_part = jnp.sum(down_all * selector[:, :, None], axis=1)
    down_part, base_keys_output = lax.optimization_barrier((down_part, base_keys_output))
    down_sum = jnp.sum(lax.all_gather(down_part, "tp"), axis=0)
    down_low = down_sum.astype(jnp.bfloat16)
    spread_rows = (selector.astype(jnp.bfloat16)[:, :, None] * down_low[:, None, :]).reshape(
        slot_total, adapter_number * rank
    )
    up_flat = adapter_up_weight.reshape(adapter_number * rank, key_feature_width)
    adapter_update = jnp.dot(spread_rows, up_flat, preferred_element_type=jnp.float32).astype(
        jnp.bfloat16
    )
    adapter_update = adapter_update.reshape(groups, slots_per_group, key_feature_width)
    rows_sent_back = lax.all_to_all(adapter_update, "ad", split_axis=0, concat_axis=0, tiled=True)
    routed = jnp.dot(
        dispatch.T,
        rows_sent_back.reshape(slot_total, key_feature_width),
        preferred_element_type=jnp.float32,
    )
    out = (base_keys_output + routed).astype(jnp.bfloat16)
    return out.reshape(step_count, row_dev, key_feature_width)


def solution(mesh):
    placed = (
        P(None, "ad", "tp"),
        P(None, "ad"),
        P("tp", None),
        P("ad", "tp", None),
        P("ad", None, "tp"),
    )
    return jax.shard_map(
        body, mesh=mesh, in_specs=placed, out_specs=P(None, "ad", "tp"), check_vma=False
    )
```

```python
import jax
import jax.numpy as jnp
from jax import lax
from jax.sharding import PartitionSpec as P

CAP = 2
TAG_WIDTH = 128


def body(tokens, row_adapter_index, key_base_weight, adapter_down_weight, adapter_up_weight):
    step_count, row_dev, width_per_shard = tokens.shape
    groups = lax.axis_size("ad")
    adapter_number = adapter_down_weight.shape[0]
    rank = adapter_down_weight.shape[2]
    row_total = step_count * row_dev
    slots_per_group = step_count * CAP
    slot_total = groups * slots_per_group

    gathered_rows = tokens.reshape(row_total, width_per_shard)
    partial_base = jnp.dot(gathered_rows, key_base_weight, preferred_element_type=jnp.float32)
    base_keys_output = lax.psum_scatter(partial_base, "tp", scatter_dimension=1, tiled=True)
    key_feature_width = base_keys_output.shape[1]

    index_list = row_adapter_index.reshape(step_count, row_dev)
    owner_group = index_list // adapter_number
    local_index = index_list % adapter_number
    group_hits = (owner_group[:, :, None] == jnp.arange(groups, dtype=jnp.int32)[None, None, :]).astype(
        jnp.int32
    )
    slot_rank = jnp.sum((jnp.cumsum(group_hits, axis=1) - group_hits) * group_hits, axis=2)
    step_ids = jnp.arange(step_count, dtype=jnp.int32)[:, None]
    slot_index = (owner_group * slots_per_group + step_ids * CAP + slot_rank).reshape(row_total)
    dispatch = (
        slot_index[None, :] == jnp.arange(slot_total, dtype=jnp.int32)[:, None]
    ).astype(jnp.bfloat16)

    tag_values = (local_index + 1).astype(jnp.bfloat16).reshape(row_total, 1)
    send_rows = jnp.dot(dispatch, gathered_rows, preferred_element_type=jnp.float32).astype(jnp.bfloat16)
    send_tags = jnp.dot(dispatch, tag_values, preferred_element_type=jnp.float32).astype(jnp.bfloat16)
    send_tags = jnp.pad(send_tags.reshape(groups, slots_per_group), ((0, 0), (0, TAG_WIDTH - slots_per_group)))
    send_all = jnp.concatenate(
        [send_rows.reshape(groups, slots_per_group * width_per_shard), send_tags], axis=1
    )
    incoming = lax.all_to_all(send_all, "ad", split_axis=0, concat_axis=0, tiled=True)
    incoming_rows = incoming[:, : slots_per_group * width_per_shard].reshape(slot_total, width_per_shard)
    incoming_labels = incoming[:, slots_per_group * width_per_shard :][:, :slots_per_group].reshape(
        slot_total
    )

    down_all = jnp.einsum(
        "nd,adr->nar", incoming_rows, adapter_down_weight, preferred_element_type=jnp.float32
    )
    labels = (jnp.arange(adapter_number, dtype=jnp.int32) + 1).astype(jnp.bfloat16)
    selector = (incoming_labels[:, None] == labels[None, :]).astype(jnp.float32)
    down_part = jnp.sum(down_all * selector[:, :, None], axis=1)
    down_sum = lax.psum(down_part, "tp")
    down_low = down_sum.astype(jnp.bfloat16)
    spread_rows = (selector.astype(jnp.bfloat16)[:, :, None] * down_low[:, None, :]).reshape(
        slot_total, adapter_number * rank
    )
    up_flat = adapter_up_weight.reshape(adapter_number * rank, key_feature_width)
    adapter_update = jnp.dot(spread_rows, up_flat, preferred_element_type=jnp.float32).astype(
        jnp.bfloat16
    )
    adapter_update = adapter_update.reshape(groups, slots_per_group, key_feature_width)
    rows_sent_back = lax.all_to_all(adapter_update, "ad", split_axis=0, concat_axis=0, tiled=True)
    routed = jnp.dot(
        dispatch.T,
        rows_sent_back.reshape(slot_total, key_feature_width),
        preferred_element_type=jnp.float32,
    )
    out = (base_keys_output + routed).astype(jnp.bfloat16)
    return out.reshape(step_count, row_dev, key_feature_width)


def solution(mesh):
    placed = (
        P(None, "ad", "tp"),
        P(None, "ad"),
        P("tp", None),
        P("ad", "tp", None),
        P("ad", None, "tp"),
    )
    return jax.shard_map(
        body, mesh=mesh, in_specs=placed, out_specs=P(None, "ad", "tp"), check_vma=False
    )
```

```python
import jax
import jax.numpy as jnp
from jax import lax
from jax.sharding import PartitionSpec as P

CAP = 2
TAG_WIDTH = 128


def body(tokens, row_adapter_index, key_base_weight, adapter_down_weight, adapter_up_weight):
    step_count, row_dev, width_per_shard = tokens.shape
    groups = lax.axis_size("ad")
    adapter_number = adapter_down_weight.shape[0]
    rank = adapter_down_weight.shape[2]
    row_total = step_count * row_dev
    slots_per_group = step_count * CAP
    slot_total = groups * slots_per_group

    gathered_rows = tokens.reshape(row_total, width_per_shard)
    partial_base = jnp.dot(gathered_rows, key_base_weight, preferred_element_type=jnp.float32)
    base_keys_output = lax.psum_scatter(partial_base, "tp", scatter_dimension=1, tiled=True)
    key_feature_width = base_keys_output.shape[1]

    index_list = row_adapter_index.reshape(step_count, row_dev)
    owner_group = index_list // adapter_number
    local_index = index_list % adapter_number
    group_hits = (owner_group[:, :, None] == jnp.arange(groups, dtype=jnp.int32)[None, None, :]).astype(
        jnp.int32
    )
    slot_rank = jnp.sum((jnp.cumsum(group_hits, axis=1) - group_hits) * group_hits, axis=2)
    step_ids = jnp.arange(step_count, dtype=jnp.int32)[:, None]
    slot_index = (owner_group * slots_per_group + step_ids * CAP + slot_rank).reshape(row_total)
    dispatch = (
        slot_index[None, :] == jnp.arange(slot_total, dtype=jnp.int32)[:, None]
    ).astype(jnp.bfloat16)

    tag_values = (local_index + 1).astype(jnp.bfloat16).reshape(row_total, 1)
    tag_block = jnp.broadcast_to(tag_values, (row_total, TAG_WIDTH))
    rows_tagged = jnp.concatenate([gathered_rows, tag_block], axis=1)
    row_of_slot = jnp.sum(
        (slot_index[None, :] == jnp.arange(slot_total, dtype=jnp.int32)[:, None]).astype(jnp.int32)
        * (jnp.arange(row_total, dtype=jnp.int32)[None, :] - row_total),
        axis=1,
    ) + row_total
    rows_padded = jnp.concatenate([rows_tagged, jnp.zeros((1, rows_tagged.shape[1]), rows_tagged.dtype)])
    send_rows = jnp.take(rows_padded, row_of_slot, axis=0, mode="clip")
    send_rows = send_rows.reshape(groups, slots_per_group, width_per_shard + TAG_WIDTH)
    incoming = lax.all_to_all(send_rows, "ad", split_axis=0, concat_axis=0, tiled=True)
    incoming = incoming.reshape(slot_total, width_per_shard + TAG_WIDTH)
    incoming_rows = incoming[:, :width_per_shard]
    incoming_labels = incoming[:, width_per_shard]

    down_all = jnp.einsum(
        "nd,adr->nar", incoming_rows, adapter_down_weight, preferred_element_type=jnp.float32
    )
    labels = (jnp.arange(adapter_number, dtype=jnp.int32) + 1).astype(jnp.bfloat16)
    selector = (incoming_labels[:, None] == labels[None, :]).astype(jnp.float32)
    down_part = jnp.sum(down_all * selector[:, :, None], axis=1)
    down_sum = lax.psum(down_part, "tp")
    down_low = down_sum.astype(jnp.bfloat16)
    spread_rows = (selector.astype(jnp.bfloat16)[:, :, None] * down_low[:, None, :]).reshape(
        slot_total, adapter_number * rank
    )
    up_flat = adapter_up_weight.reshape(adapter_number * rank, key_feature_width)
    adapter_update = jnp.dot(spread_rows, up_flat, preferred_element_type=jnp.float32).astype(
        jnp.bfloat16
    )
    adapter_update = adapter_update.reshape(groups, slots_per_group, key_feature_width)
    rows_sent_back = lax.all_to_all(adapter_update, "ad", split_axis=0, concat_axis=0, tiled=True)
    routed = jnp.dot(
        dispatch.T,
        rows_sent_back.reshape(slot_total, key_feature_width),
        preferred_element_type=jnp.float32,
    )
    out = (base_keys_output + routed).astype(jnp.bfloat16)
    return out.reshape(step_count, row_dev, key_feature_width)


def solution(mesh):
    placed = (
        P(None, "ad", "tp"),
        P(None, "ad"),
        P("tp", None),
        P("ad", "tp", None),
        P("ad", None, "tp"),
    )
    return jax.shard_map(
        body, mesh=mesh, in_specs=placed, out_specs=P(None, "ad", "tp"), check_vma=False
    )
```

```python
import jax
import jax.numpy as jnp
from jax import lax
from jax.sharding import PartitionSpec as P

CAP = 2
TAG_WIDTH = 128


def body(tokens, row_adapter_index, key_base_weight, adapter_down_weight, adapter_up_weight):
    step_count, row_dev, width_per_shard = tokens.shape
    groups = lax.axis_size("ad")
    adapter_number = adapter_down_weight.shape[0]
    rank = adapter_down_weight.shape[2]
    row_total = step_count * row_dev
    slots_per_group = step_count * CAP
    slot_total = groups * slots_per_group

    gathered_rows = tokens.reshape(row_total, width_per_shard)
    partial_base = jnp.dot(gathered_rows, key_base_weight, preferred_element_type=jnp.float32)
    base_keys_output = lax.psum_scatter(partial_base, "tp", scatter_dimension=1, tiled=True)
    key_feature_width = base_keys_output.shape[1]

    index_list = row_adapter_index.reshape(step_count, row_dev)
    owner_group = index_list // adapter_number
    local_index = index_list % adapter_number
    group_hits = (owner_group[:, :, None] == jnp.arange(groups, dtype=jnp.int32)[None, None, :]).astype(
        jnp.int32
    )
    slot_rank = jnp.sum((jnp.cumsum(group_hits, axis=1) - group_hits) * group_hits, axis=2)
    step_ids = jnp.arange(step_count, dtype=jnp.int32)[:, None]
    slot_index = (owner_group * slots_per_group + step_ids * CAP + slot_rank).reshape(row_total)
    dispatch = (
        slot_index[None, :] == jnp.arange(slot_total, dtype=jnp.int32)[:, None]
    ).astype(jnp.bfloat16)

    tag_values = (local_index + 1).astype(jnp.bfloat16).reshape(row_total, 1)
    tag_block = jnp.broadcast_to(tag_values, (row_total, TAG_WIDTH))
    rows_tagged = jnp.concatenate([gathered_rows, tag_block], axis=1)
    send_rows = jnp.dot(dispatch, rows_tagged, preferred_element_type=jnp.float32).astype(jnp.bfloat16)
    send_rows = send_rows.reshape(groups, slots_per_group, width_per_shard + TAG_WIDTH)
    incoming = lax.all_to_all(send_rows, "ad", split_axis=0, concat_axis=0, tiled=True)
    incoming = incoming.reshape(slot_total, width_per_shard + TAG_WIDTH)
    incoming_rows = incoming[:, :width_per_shard]
    incoming_labels = incoming[:, width_per_shard]

    down_all = jnp.einsum(
        "nd,adr->nar", incoming_rows, adapter_down_weight, preferred_element_type=jnp.float32
    )
    labels = (jnp.arange(adapter_number, dtype=jnp.int32) + 1).astype(jnp.bfloat16)
    selector = (incoming_labels[:, None] == labels[None, :]).astype(jnp.float32)
    down_part = jnp.sum(down_all * selector[:, :, None], axis=1)
    shards = lax.axis_size("tp")
    chunks = down_part.reshape(shards, slot_total // shards, rank)
    chunk_sum = jnp.sum(lax.all_to_all(chunks, "tp", split_axis=0, concat_axis=0, tiled=True), axis=0)
    spread = jnp.broadcast_to(chunk_sum[None], (shards,) + chunk_sum.shape)
    down_sum = lax.all_to_all(spread, "tp", split_axis=0, concat_axis=0, tiled=True).reshape(
        slot_total, rank
    )
    down_low = down_sum.astype(jnp.bfloat16)
    spread_rows = (selector.astype(jnp.bfloat16)[:, :, None] * down_low[:, None, :]).reshape(
        slot_total, adapter_number * rank
    )
    up_flat = adapter_up_weight.reshape(adapter_number * rank, key_feature_width)
    adapter_update = jnp.dot(spread_rows, up_flat, preferred_element_type=jnp.float32).astype(
        jnp.bfloat16
    )
    adapter_update = adapter_update.reshape(groups, slots_per_group, key_feature_width)
    rows_sent_back = lax.all_to_all(adapter_update, "ad", split_axis=0, concat_axis=0, tiled=True)
    routed = jnp.dot(
        dispatch.T,
        rows_sent_back.reshape(slot_total, key_feature_width),
        preferred_element_type=jnp.float32,
    )
    out = (base_keys_output + routed).astype(jnp.bfloat16)
    return out.reshape(step_count, row_dev, key_feature_width)


def solution(mesh):
    placed = (
        P(None, "ad", "tp"),
        P(None, "ad"),
        P("tp", None),
        P("ad", "tp", None),
        P("ad", None, "tp"),
    )
    return jax.shard_map(
        body, mesh=mesh, in_specs=placed, out_specs=P(None, "ad", "tp"), check_vma=False
    )
```

```python
import jax
import jax.numpy as jnp
from jax import lax
from jax.sharding import PartitionSpec as P

CAP = 2
TAG_WIDTH = 128


def body(tokens, row_adapter_index, key_base_weight, adapter_down_weight, adapter_up_weight):
    step_count, row_dev, width_per_shard = tokens.shape
    groups = lax.axis_size("ad")
    adapter_number = adapter_down_weight.shape[0]
    rank = adapter_down_weight.shape[2]
    row_total = step_count * row_dev
    slots_per_group = step_count * CAP
    slot_total = groups * slots_per_group

    gathered_rows = tokens.reshape(row_total, width_per_shard)
    partial_base = jnp.dot(gathered_rows, key_base_weight, preferred_element_type=jnp.float32)
    tp_size = lax.axis_size("tp")
    key_feature_width = partial_base.shape[1] // tp_size
    base_pieces = partial_base.reshape(row_total, tp_size, key_feature_width).transpose(1, 0, 2)
    base_keys_output = jnp.sum(
        lax.all_to_all(base_pieces, "tp", split_axis=0, concat_axis=0, tiled=True), axis=0
    )

    index_list = row_adapter_index.reshape(step_count, row_dev)
    owner_group = index_list // adapter_number
    local_index = index_list % adapter_number
    group_hits = (owner_group[:, :, None] == jnp.arange(groups, dtype=jnp.int32)[None, None, :]).astype(
        jnp.int32
    )
    slot_rank = jnp.sum((jnp.cumsum(group_hits, axis=1) - group_hits) * group_hits, axis=2)
    step_ids = jnp.arange(step_count, dtype=jnp.int32)[:, None]
    slot_index = (owner_group * slots_per_group + step_ids * CAP + slot_rank).reshape(row_total)
    dispatch = (
        slot_index[None, :] == jnp.arange(slot_total, dtype=jnp.int32)[:, None]
    ).astype(jnp.bfloat16)

    tag_values = (local_index + 1).astype(jnp.bfloat16).reshape(row_total, 1)
    tag_block = jnp.broadcast_to(tag_values, (row_total, TAG_WIDTH))
    rows_tagged = jnp.concatenate([gathered_rows, tag_block], axis=1)
    send_rows = jnp.dot(dispatch, rows_tagged, preferred_element_type=jnp.float32).astype(jnp.bfloat16)
    send_rows = send_rows.reshape(groups, slots_per_group, width_per_shard + TAG_WIDTH)
    incoming = lax.all_to_all(send_rows, "ad", split_axis=0, concat_axis=0, tiled=True)
    incoming, base_keys_output = lax.optimization_barrier((incoming, base_keys_output))
    incoming = incoming.reshape(slot_total, width_per_shard + TAG_WIDTH)
    incoming_rows = incoming[:, :width_per_shard]
    incoming_labels = incoming[:, width_per_shard]

    down_all = jnp.einsum(
        "nd,adr->nar", incoming_rows, adapter_down_weight, preferred_element_type=jnp.float32
    )
    labels = (jnp.arange(adapter_number, dtype=jnp.int32) + 1).astype(jnp.bfloat16)
    selector = (incoming_labels[:, None] == labels[None, :]).astype(jnp.float32)
    down_part = jnp.sum(down_all * selector[:, :, None], axis=1)
    shards = lax.axis_size("tp")
    chunks = down_part.reshape(shards, slot_total // shards, rank)
    chunk_sum = jnp.sum(lax.all_to_all(chunks, "tp", split_axis=0, concat_axis=0, tiled=True), axis=0)
    spread = jnp.broadcast_to(chunk_sum[None], (shards,) + chunk_sum.shape)
    down_sum = lax.all_to_all(spread, "tp", split_axis=0, concat_axis=0, tiled=True).reshape(
        slot_total, rank
    )
    down_low = down_sum.astype(jnp.bfloat16)
    spread_rows = (selector.astype(jnp.bfloat16)[:, :, None] * down_low[:, None, :]).reshape(
        slot_total, adapter_number * rank
    )
    up_flat = adapter_up_weight.reshape(adapter_number * rank, key_feature_width)
    adapter_update = jnp.dot(spread_rows, up_flat, preferred_element_type=jnp.float32).astype(
        jnp.bfloat16
    )
    adapter_update = adapter_update.reshape(groups, slots_per_group, key_feature_width)
    rows_sent_back = lax.all_to_all(adapter_update, "ad", split_axis=0, concat_axis=0, tiled=True)
    routed = jnp.dot(
        dispatch.T,
        rows_sent_back.reshape(slot_total, key_feature_width),
        preferred_element_type=jnp.float32,
    )
    out = (base_keys_output + routed).astype(jnp.bfloat16)
    return out.reshape(step_count, row_dev, key_feature_width)


def solution(mesh):
    placed = (
        P(None, "ad", "tp"),
        P(None, "ad"),
        P("tp", None),
        P("ad", "tp", None),
        P("ad", None, "tp"),
    )
    return jax.shard_map(
        body, mesh=mesh, in_specs=placed, out_specs=P(None, "ad", "tp"), check_vma=False
    )
```

```python
import jax
import jax.numpy as jnp
from jax import lax
from jax.sharding import PartitionSpec as P

CAP = 2
TAG_WIDTH = 128


def body(tokens, row_adapter_index, key_base_weight, adapter_down_weight, adapter_up_weight):
    step_count, row_dev, width_per_shard = tokens.shape
    groups = lax.axis_size("ad")
    adapter_number = adapter_down_weight.shape[0]
    rank = adapter_down_weight.shape[2]
    row_total = step_count * row_dev
    slots_per_group = step_count * CAP
    slot_total = groups * slots_per_group

    gathered_rows = tokens.reshape(row_total, width_per_shard)
    tp_size = lax.axis_size("tp")
    key_feature_width = key_base_weight.shape[1] // tp_size
    base_pieces = jnp.einsum(
        "nd,dkf->knf",
        gathered_rows,
        key_base_weight.reshape(width_per_shard, tp_size, key_feature_width),
        preferred_element_type=jnp.float32,
    )
    base_keys_output = jnp.sum(
        lax.all_to_all(base_pieces, "tp", split_axis=0, concat_axis=0, tiled=True), axis=0
    )

    index_list = row_adapter_index.reshape(step_count, row_dev)
    owner_group = index_list // adapter_number
    local_index = index_list % adapter_number
    group_hits = (owner_group[:, :, None] == jnp.arange(groups, dtype=jnp.int32)[None, None, :]).astype(
        jnp.int32
    )
    slot_rank = jnp.sum((jnp.cumsum(group_hits, axis=1) - group_hits) * group_hits, axis=2)
    step_ids = jnp.arange(step_count, dtype=jnp.int32)[:, None]
    slot_index = (owner_group * slots_per_group + step_ids * CAP + slot_rank).reshape(row_total)
    dispatch = (
        slot_index[None, :] == jnp.arange(slot_total, dtype=jnp.int32)[:, None]
    ).astype(jnp.bfloat16)

    tag_values = (local_index + 1).astype(jnp.bfloat16).reshape(row_total, 1)
    tag_block = jnp.broadcast_to(tag_values, (row_total, TAG_WIDTH))
    rows_tagged = jnp.concatenate([gathered_rows, tag_block], axis=1)
    send_rows = jnp.dot(dispatch, rows_tagged, preferred_element_type=jnp.float32).astype(jnp.bfloat16)
    send_rows = send_rows.reshape(groups, slots_per_group, width_per_shard + TAG_WIDTH)
    incoming = lax.all_to_all(send_rows, "ad", split_axis=0, concat_axis=0, tiled=True)
    incoming, base_keys_output = lax.optimization_barrier((incoming, base_keys_output))
    incoming = incoming.reshape(slot_total, width_per_shard + TAG_WIDTH)
    incoming_rows = incoming[:, :width_per_shard]
    incoming_labels = incoming[:, width_per_shard]

    down_all = jnp.einsum(
        "nd,adr->nar", incoming_rows, adapter_down_weight, preferred_element_type=jnp.float32
    )
    labels = (jnp.arange(adapter_number, dtype=jnp.int32) + 1).astype(jnp.bfloat16)
    selector = (incoming_labels[:, None] == labels[None, :]).astype(jnp.float32)
    down_part = jnp.sum(down_all * selector[:, :, None], axis=1)
    shards = lax.axis_size("tp")
    chunks = down_part.reshape(shards, slot_total // shards, rank)
    chunk_sum = jnp.sum(lax.all_to_all(chunks, "tp", split_axis=0, concat_axis=0, tiled=True), axis=0)
    spread = jnp.broadcast_to(chunk_sum[None], (shards,) + chunk_sum.shape)
    down_sum = lax.all_to_all(spread, "tp", split_axis=0, concat_axis=0, tiled=True).reshape(
        slot_total, rank
    )
    down_low = down_sum.astype(jnp.bfloat16)
    spread_rows = (selector.astype(jnp.bfloat16)[:, :, None] * down_low[:, None, :]).reshape(
        slot_total, adapter_number * rank
    )
    up_flat = adapter_up_weight.reshape(adapter_number * rank, key_feature_width)
    adapter_update = jnp.dot(spread_rows, up_flat, preferred_element_type=jnp.float32).astype(
        jnp.bfloat16
    )
    adapter_update = adapter_update.reshape(groups, slots_per_group, key_feature_width)
    rows_sent_back = lax.all_to_all(adapter_update, "ad", split_axis=0, concat_axis=0, tiled=True)
    routed = jnp.dot(
        dispatch.T,
        rows_sent_back.reshape(slot_total, key_feature_width),
        preferred_element_type=jnp.float32,
    )
    out = (base_keys_output + routed).astype(jnp.bfloat16)
    return out.reshape(step_count, row_dev, key_feature_width)


def solution(mesh):
    placed = (
        P(None, "ad", "tp"),
        P(None, "ad"),
        P("tp", None),
        P("ad", "tp", None),
        P("ad", None, "tp"),
    )
    return jax.shard_map(
        body, mesh=mesh, in_specs=placed, out_specs=P(None, "ad", "tp"), check_vma=False
    )
```

```python
import jax
import jax.numpy as jnp
from jax import lax
from jax.sharding import PartitionSpec as P

CAP = 2
TAG_WIDTH = 128


def body(tokens, row_adapter_index, key_base_weight, adapter_down_weight, adapter_up_weight):
    step_count, row_dev, width_per_shard = tokens.shape
    groups = lax.axis_size("ad")
    adapter_number = adapter_down_weight.shape[0]
    rank = adapter_down_weight.shape[2]
    row_total = step_count * row_dev
    slots_per_group = step_count * CAP
    slot_total = groups * slots_per_group

    gathered_rows = tokens.reshape(row_total, width_per_shard)
    partial_base = jnp.dot(gathered_rows, key_base_weight, preferred_element_type=jnp.float32)
    tp_size = lax.axis_size("tp")
    key_feature_width = partial_base.shape[1] // tp_size
    base_pieces = partial_base.reshape(row_total, tp_size, key_feature_width).transpose(1, 0, 2)

    index_list = row_adapter_index.reshape(step_count, row_dev)
    owner_group = index_list // adapter_number
    local_index = index_list % adapter_number
    group_hits = (owner_group[:, :, None] == jnp.arange(groups, dtype=jnp.int32)[None, None, :]).astype(
        jnp.int32
    )
    slot_rank = jnp.sum((jnp.cumsum(group_hits, axis=1) - group_hits) * group_hits, axis=2)
    step_ids = jnp.arange(step_count, dtype=jnp.int32)[:, None]
    slot_index = (owner_group * slots_per_group + step_ids * CAP + slot_rank).reshape(row_total)
    dispatch = (
        slot_index[None, :] == jnp.arange(slot_total, dtype=jnp.int32)[:, None]
    ).astype(jnp.bfloat16)

    tag_values = (local_index + 1).astype(jnp.bfloat16).reshape(row_total, 1)
    tag_block = jnp.broadcast_to(tag_values, (row_total, TAG_WIDTH))
    rows_tagged = jnp.concatenate([gathered_rows, tag_block], axis=1)
    send_rows = jnp.dot(dispatch, rows_tagged, preferred_element_type=jnp.float32).astype(jnp.bfloat16)
    send_rows = send_rows.reshape(groups, slots_per_group, width_per_shard + TAG_WIDTH)
    incoming = lax.all_to_all(send_rows, "ad", split_axis=0, concat_axis=0, tiled=True)
    incoming = incoming.reshape(slot_total, width_per_shard + TAG_WIDTH)
    incoming_rows = incoming[:, :width_per_shard]
    incoming_labels = incoming[:, width_per_shard]

    down_all = jnp.einsum(
        "nd,adr->nar", incoming_rows, adapter_down_weight, preferred_element_type=jnp.float32
    )
    labels = (jnp.arange(adapter_number, dtype=jnp.int32) + 1).astype(jnp.bfloat16)
    selector = (incoming_labels[:, None] == labels[None, :]).astype(jnp.float32)
    down_part = jnp.sum(down_all * selector[:, :, None], axis=1)
    shards = lax.axis_size("tp")
    chunk_width = slot_total // shards * rank
    chunks = jnp.concatenate(
        [down_part.reshape(shards, chunk_width), base_pieces.reshape(shards, -1)], axis=1
    )
    moved = lax.all_to_all(chunks, "tp", split_axis=0, concat_axis=0, tiled=True)
    chunk_sum = jnp.sum(moved[:, :chunk_width], axis=0).reshape(slot_total // shards, rank)
    base_keys_output = jnp.sum(
        moved[:, chunk_width:].reshape(shards, row_total, key_feature_width), axis=0
    )
    spread = jnp.broadcast_to(chunk_sum[None], (shards,) + chunk_sum.shape)
    down_sum = lax.all_to_all(spread, "tp", split_axis=0, concat_axis=0, tiled=True).reshape(
        slot_total, rank
    )
    down_low = down_sum.astype(jnp.bfloat16)
    spread_rows = (selector.astype(jnp.bfloat16)[:, :, None] * down_low[:, None, :]).reshape(
        slot_total, adapter_number * rank
    )
    up_flat = adapter_up_weight.reshape(adapter_number * rank, key_feature_width)
    adapter_update = jnp.dot(spread_rows, up_flat, preferred_element_type=jnp.float32).astype(
        jnp.bfloat16
    )
    adapter_update = adapter_update.reshape(groups, slots_per_group, key_feature_width)
    rows_sent_back = lax.all_to_all(adapter_update, "ad", split_axis=0, concat_axis=0, tiled=True)
    routed = jnp.dot(
        dispatch.T,
        rows_sent_back.reshape(slot_total, key_feature_width),
        preferred_element_type=jnp.float32,
    )
    out = (base_keys_output + routed).astype(jnp.bfloat16)
    return out.reshape(step_count, row_dev, key_feature_width)


def solution(mesh):
    placed = (
        P(None, "ad", "tp"),
        P(None, "ad"),
        P("tp", None),
        P("ad", "tp", None),
        P("ad", None, "tp"),
    )
    return jax.shard_map(
        body, mesh=mesh, in_specs=placed, out_specs=P(None, "ad", "tp"), check_vma=False
    )
```

```python
import jax
import jax.numpy as jnp
from jax import lax
from jax.sharding import PartitionSpec as P

CAP = 2
TAG_WIDTH = 128


def body(tokens, row_adapter_index, key_base_weight, adapter_down_weight, adapter_up_weight):
    step_count, row_dev, width_per_shard = tokens.shape
    groups = lax.axis_size("ad")
    adapter_number = adapter_down_weight.shape[0]
    rank = adapter_down_weight.shape[2]
    row_total = step_count * row_dev
    slots_per_group = step_count * CAP
    slot_total = groups * slots_per_group

    gathered_rows = tokens.reshape(row_total, width_per_shard)
    partial_base = jnp.dot(gathered_rows, key_base_weight, preferred_element_type=jnp.float32)
    tp_size = lax.axis_size("tp")
    key_feature_width = partial_base.shape[1] // tp_size
    base_pieces = partial_base.reshape(row_total, tp_size, key_feature_width).transpose(1, 0, 2)

    index_list = row_adapter_index.reshape(step_count, row_dev)
    owner_group = index_list // adapter_number
    local_index = index_list % adapter_number
    group_hits = (owner_group[:, :, None] == jnp.arange(groups, dtype=jnp.int32)[None, None, :]).astype(
        jnp.int32
    )
    slot_rank = jnp.sum((jnp.cumsum(group_hits, axis=1) - group_hits) * group_hits, axis=2)
    step_ids = jnp.arange(step_count, dtype=jnp.int32)[:, None]
    slot_index = (owner_group * slots_per_group + step_ids * CAP + slot_rank).reshape(row_total)
    dispatch = (
        slot_index[None, :] == jnp.arange(slot_total, dtype=jnp.int32)[:, None]
    ).astype(jnp.bfloat16)

    tag_values = (local_index + 1).astype(jnp.bfloat16).reshape(row_total, 1)
    tag_block = jnp.broadcast_to(tag_values, (row_total, TAG_WIDTH))
    rows_tagged = jnp.concatenate([gathered_rows, tag_block], axis=1)
    send_rows = jnp.dot(dispatch, rows_tagged, preferred_element_type=jnp.float32).astype(jnp.bfloat16)
    send_rows = send_rows.reshape(groups, slots_per_group, width_per_shard + TAG_WIDTH)
    incoming = lax.all_to_all(send_rows, "ad", split_axis=0, concat_axis=0, tiled=True)
    incoming = incoming.reshape(slot_total, width_per_shard + TAG_WIDTH)
    incoming_rows = incoming[:, :width_per_shard]
    incoming_labels = incoming[:, width_per_shard]

    down_all = jnp.einsum(
        "nd,adr->nar", incoming_rows, adapter_down_weight, preferred_element_type=jnp.float32
    )
    labels = (jnp.arange(adapter_number, dtype=jnp.int32) + 1).astype(jnp.bfloat16)
    selector = (incoming_labels[:, None] == labels[None, :]).astype(jnp.float32)
    down_part = jnp.sum(down_all * selector[:, :, None], axis=1)
    shards = lax.axis_size("tp")
    chunk_width = slot_total // shards * rank
    down_flat = down_part.reshape(shards, chunk_width)
    down_high = down_flat.astype(jnp.bfloat16)
    down_low_part = (down_flat - down_high.astype(jnp.float32)).astype(jnp.bfloat16)
    chunks = jnp.concatenate(
        [down_high, down_low_part, base_pieces.reshape(shards, -1).astype(jnp.bfloat16)], axis=1
    )
    moved = lax.all_to_all(chunks, "tp", split_axis=0, concat_axis=0, tiled=True).astype(jnp.float32)
    chunk_sum = jnp.sum(
        moved[:, :chunk_width] + moved[:, chunk_width : 2 * chunk_width], axis=0
    ).reshape(slot_total // shards, rank)
    base_keys_output = jnp.sum(
        moved[:, 2 * chunk_width :].reshape(shards, row_total, key_feature_width), axis=0
    )
    spread = jnp.broadcast_to(chunk_sum[None], (shards,) + chunk_sum.shape)
    down_sum = lax.all_to_all(spread, "tp", split_axis=0, concat_axis=0, tiled=True).reshape(
        slot_total, rank
    )
    down_low = down_sum.astype(jnp.bfloat16)
    spread_rows = (selector.astype(jnp.bfloat16)[:, :, None] * down_low[:, None, :]).reshape(
        slot_total, adapter_number * rank
    )
    up_flat = adapter_up_weight.reshape(adapter_number * rank, key_feature_width)
    adapter_update = jnp.dot(spread_rows, up_flat, preferred_element_type=jnp.float32).astype(
        jnp.bfloat16
    )
    adapter_update = adapter_update.reshape(groups, slots_per_group, key_feature_width)
    rows_sent_back = lax.all_to_all(adapter_update, "ad", split_axis=0, concat_axis=0, tiled=True)
    routed = jnp.dot(
        dispatch.T,
        rows_sent_back.reshape(slot_total, key_feature_width),
        preferred_element_type=jnp.float32,
    )
    out = (base_keys_output + routed).astype(jnp.bfloat16)
    return out.reshape(step_count, row_dev, key_feature_width)


def solution(mesh):
    placed = (
        P(None, "ad", "tp"),
        P(None, "ad"),
        P("tp", None),
        P("ad", "tp", None),
        P("ad", None, "tp"),
    )
    return jax.shard_map(
        body, mesh=mesh, in_specs=placed, out_specs=P(None, "ad", "tp"), check_vma=False
    )
```

```python
import jax
import jax.numpy as jnp
from jax import lax
from jax.sharding import PartitionSpec as P

CAP = 2
TAG_WIDTH = 128


def body(tokens, row_adapter_index, key_base_weight, adapter_down_weight, adapter_up_weight):
    step_count, row_dev, width_per_shard = tokens.shape
    groups = lax.axis_size("ad")
    adapter_number = adapter_down_weight.shape[0]
    rank = adapter_down_weight.shape[2]
    row_total = step_count * row_dev
    slots_per_group = step_count * CAP
    slot_total = groups * slots_per_group

    gathered_rows = tokens.reshape(row_total, width_per_shard)
    partial_base = jnp.dot(gathered_rows, key_base_weight, preferred_element_type=jnp.float32)
    tp_size = lax.axis_size("tp")
    key_feature_width = partial_base.shape[1] // tp_size
    base_pieces = partial_base.reshape(row_total, tp_size, key_feature_width).transpose(1, 0, 2)
    half_rows = row_total // 2
    base_halves = base_pieces.reshape(tp_size, 2, half_rows, key_feature_width)
    core = lax.axis_index("tp") % 2
    keep = lax.dynamic_index_in_dim(base_halves, core, axis=1, keepdims=False)
    give = lax.dynamic_index_in_dim(base_halves, 1 - core, axis=1, keepdims=False)
    pair_sum = keep + lax.ppermute(give, "tp", [(k, k ^ 1) for k in range(tp_size)])

    index_list = row_adapter_index.reshape(step_count, row_dev)
    owner_group = index_list // adapter_number
    local_index = index_list % adapter_number
    group_hits = (owner_group[:, :, None] == jnp.arange(groups, dtype=jnp.int32)[None, None, :]).astype(
        jnp.int32
    )
    slot_rank = jnp.sum((jnp.cumsum(group_hits, axis=1) - group_hits) * group_hits, axis=2)
    step_ids = jnp.arange(step_count, dtype=jnp.int32)[:, None]
    slot_index = (owner_group * slots_per_group + step_ids * CAP + slot_rank).reshape(row_total)
    dispatch = (
        slot_index[None, :] == jnp.arange(slot_total, dtype=jnp.int32)[:, None]
    ).astype(jnp.bfloat16)

    tag_values = (local_index + 1).astype(jnp.bfloat16).reshape(row_total, 1)
    tag_block = jnp.broadcast_to(tag_values, (row_total, TAG_WIDTH))
    rows_tagged = jnp.concatenate([gathered_rows, tag_block], axis=1)
    send_rows = jnp.dot(dispatch, rows_tagged, preferred_element_type=jnp.float32).astype(jnp.bfloat16)
    send_rows = send_rows.reshape(groups, slots_per_group, width_per_shard + TAG_WIDTH)
    incoming = lax.all_to_all(send_rows, "ad", split_axis=0, concat_axis=0, tiled=True)
    incoming = incoming.reshape(slot_total, width_per_shard + TAG_WIDTH)
    incoming_rows = incoming[:, :width_per_shard]
    incoming_labels = incoming[:, width_per_shard]

    down_all = jnp.einsum(
        "nd,adr->nar", incoming_rows, adapter_down_weight, preferred_element_type=jnp.float32
    )
    labels = (jnp.arange(adapter_number, dtype=jnp.int32) + 1).astype(jnp.bfloat16)
    selector = (incoming_labels[:, None] == labels[None, :]).astype(jnp.float32)
    down_part = jnp.sum(down_all * selector[:, :, None], axis=1)
    shards = lax.axis_size("tp")
    chunk_width = slot_total // shards * rank
    chunks = jnp.concatenate(
        [down_part.reshape(shards, chunk_width), pair_sum.reshape(shards, -1)], axis=1
    )
    moved = lax.all_to_all(chunks, "tp", split_axis=0, concat_axis=0, tiled=True)
    chunk_sum = jnp.sum(moved[:, :chunk_width], axis=0).reshape(slot_total // shards, rank)
    base_keys_output = jnp.sum(
        moved[:, chunk_width:].reshape(shards // 2, 2, half_rows, key_feature_width), axis=0
    ).reshape(row_total, key_feature_width)
    spread = jnp.broadcast_to(chunk_sum[None], (shards,) + chunk_sum.shape)
    down_sum = lax.all_to_all(spread, "tp", split_axis=0, concat_axis=0, tiled=True).reshape(
        slot_total, rank
    )
    down_low = down_sum.astype(jnp.bfloat16)
    spread_rows = (selector.astype(jnp.bfloat16)[:, :, None] * down_low[:, None, :]).reshape(
        slot_total, adapter_number * rank
    )
    up_flat = adapter_up_weight.reshape(adapter_number * rank, key_feature_width)
    adapter_update = jnp.dot(spread_rows, up_flat, preferred_element_type=jnp.float32).astype(
        jnp.bfloat16
    )
    adapter_update = adapter_update.reshape(groups, slots_per_group, key_feature_width)
    rows_sent_back = lax.all_to_all(adapter_update, "ad", split_axis=0, concat_axis=0, tiled=True)
    routed = jnp.dot(
        dispatch.T,
        rows_sent_back.reshape(slot_total, key_feature_width),
        preferred_element_type=jnp.float32,
    )
    out = (base_keys_output + routed).astype(jnp.bfloat16)
    return out.reshape(step_count, row_dev, key_feature_width)


def solution(mesh):
    placed = (
        P(None, "ad", "tp"),
        P(None, "ad"),
        P("tp", None),
        P("ad", "tp", None),
        P("ad", None, "tp"),
    )
    return jax.shard_map(
        body, mesh=mesh, in_specs=placed, out_specs=P(None, "ad", "tp"), check_vma=False
    )
```

```python
import jax
import jax.numpy as jnp
from jax import lax
from jax.sharding import PartitionSpec as P

CAP = 2
TAG_WIDTH = 128


def body(tokens, row_adapter_index, key_base_weight, adapter_down_weight, adapter_up_weight):
    step_count, row_dev, width_per_shard = tokens.shape
    groups = lax.axis_size("ad")
    adapter_number = adapter_down_weight.shape[0]
    rank = adapter_down_weight.shape[2]
    row_total = step_count * row_dev
    slots_per_group = step_count * CAP
    slot_total = groups * slots_per_group

    gathered_rows = tokens.reshape(row_total, width_per_shard)
    partial_base = jnp.dot(gathered_rows, key_base_weight, preferred_element_type=jnp.float32)
    tp_size = lax.axis_size("tp")
    key_feature_width = partial_base.shape[1] // tp_size
    base_pieces = partial_base.reshape(row_total, tp_size, key_feature_width).transpose(1, 0, 2)
    tp_index = lax.axis_index("tp")
    base_left = base_pieces
    bit = 1
    while bit < tp_size:
        base_left = base_left.reshape(base_left.shape[0] // 2, 2, row_total, key_feature_width)
        side = (tp_index // bit) % 2
        keep = lax.dynamic_index_in_dim(base_left, side, axis=1, keepdims=False)
        give = lax.dynamic_index_in_dim(base_left, 1 - side, axis=1, keepdims=False)
        base_left = keep + lax.ppermute(give, "tp", [(k, k ^ bit) for k in range(tp_size)])
        bit *= 2
    base_keys_output = base_left.reshape(row_total, key_feature_width)

    index_list = row_adapter_index.reshape(step_count, row_dev)
    owner_group = index_list // adapter_number
    local_index = index_list % adapter_number
    group_hits = (owner_group[:, :, None] == jnp.arange(groups, dtype=jnp.int32)[None, None, :]).astype(
        jnp.int32
    )
    slot_rank = jnp.sum((jnp.cumsum(group_hits, axis=1) - group_hits) * group_hits, axis=2)
    step_ids = jnp.arange(step_count, dtype=jnp.int32)[:, None]
    slot_index = (owner_group * slots_per_group + step_ids * CAP + slot_rank).reshape(row_total)
    dispatch = (
        slot_index[None, :] == jnp.arange(slot_total, dtype=jnp.int32)[:, None]
    ).astype(jnp.bfloat16)

    tag_values = (local_index + 1).astype(jnp.bfloat16).reshape(row_total, 1)
    tag_block = jnp.broadcast_to(tag_values, (row_total, TAG_WIDTH))
    rows_tagged = jnp.concatenate([gathered_rows, tag_block], axis=1)
    send_rows = jnp.dot(dispatch, rows_tagged, preferred_element_type=jnp.float32).astype(jnp.bfloat16)
    send_rows = send_rows.reshape(groups, slots_per_group, width_per_shard + TAG_WIDTH)
    incoming = lax.all_to_all(send_rows, "ad", split_axis=0, concat_axis=0, tiled=True)
    incoming = incoming.reshape(slot_total, width_per_shard + TAG_WIDTH)
    incoming_rows = incoming[:, :width_per_shard]
    incoming_labels = incoming[:, width_per_shard]

    down_all = jnp.einsum(
        "nd,adr->nar", incoming_rows, adapter_down_weight, preferred_element_type=jnp.float32
    )
    labels = (jnp.arange(adapter_number, dtype=jnp.int32) + 1).astype(jnp.bfloat16)
    selector = (incoming_labels[:, None] == labels[None, :]).astype(jnp.float32)
    down_part = jnp.sum(down_all * selector[:, :, None], axis=1)
    shards = lax.axis_size("tp")
    chunk_width = slot_total // shards * rank
    chunks = down_part.reshape(shards, slot_total // shards, rank)
    chunk_sum = jnp.sum(lax.all_to_all(chunks, "tp", split_axis=0, concat_axis=0, tiled=True), axis=0)
    spread = jnp.broadcast_to(chunk_sum[None], (shards,) + chunk_sum.shape)
    down_sum = lax.all_to_all(spread, "tp", split_axis=0, concat_axis=0, tiled=True).reshape(
        slot_total, rank
    )
    down_low = down_sum.astype(jnp.bfloat16)
    spread_rows = (selector.astype(jnp.bfloat16)[:, :, None] * down_low[:, None, :]).reshape(
        slot_total, adapter_number * rank
    )
    up_flat = adapter_up_weight.reshape(adapter_number * rank, key_feature_width)
    adapter_update = jnp.dot(spread_rows, up_flat, preferred_element_type=jnp.float32).astype(
        jnp.bfloat16
    )
    adapter_update = adapter_update.reshape(groups, slots_per_group, key_feature_width)
    rows_sent_back = lax.all_to_all(adapter_update, "ad", split_axis=0, concat_axis=0, tiled=True)
    routed = jnp.dot(
        dispatch.T,
        rows_sent_back.reshape(slot_total, key_feature_width),
        preferred_element_type=jnp.float32,
    )
    out = (base_keys_output + routed).astype(jnp.bfloat16)
    return out.reshape(step_count, row_dev, key_feature_width)


def solution(mesh):
    placed = (
        P(None, "ad", "tp"),
        P(None, "ad"),
        P("tp", None),
        P("ad", "tp", None),
        P("ad", None, "tp"),
    )
    return jax.shard_map(
        body, mesh=mesh, in_specs=placed, out_specs=P(None, "ad", "tp"), check_vma=False
    )
```

```python
import jax
import jax.numpy as jnp
from jax import lax
from jax.sharding import PartitionSpec as P

CAP = 2
TAG_WIDTH = 128


def body(tokens, row_adapter_index, key_base_weight, adapter_down_weight, adapter_up_weight):
    step_count, row_dev, width_per_shard = tokens.shape
    groups = lax.axis_size("ad")
    adapter_number = adapter_down_weight.shape[0]
    rank = adapter_down_weight.shape[2]
    row_total = step_count * row_dev
    slots_per_group = step_count * CAP
    slot_total = groups * slots_per_group

    gathered_rows = tokens.reshape(row_total, width_per_shard)
    partial_base = jnp.dot(gathered_rows, key_base_weight, preferred_element_type=jnp.float32)
    tp_size = lax.axis_size("tp")
    key_feature_width = partial_base.shape[1] // tp_size
    base_pieces = partial_base.reshape(row_total, tp_size, key_feature_width).transpose(1, 0, 2)
    tp_index = lax.axis_index("tp")
    base_left = base_pieces
    bit = 1
    while bit < tp_size:
        base_left = base_left.reshape(base_left.shape[0] // 2, 2, row_total, key_feature_width)
        side = (tp_index // bit) % 2
        keep = lax.dynamic_index_in_dim(base_left, side, axis=1, keepdims=False)
        give = lax.dynamic_index_in_dim(base_left, 1 - side, axis=1, keepdims=False)
        base_left = keep + lax.ppermute(give, "tp", [(k, k ^ bit) for k in range(tp_size)])
        bit *= 2
    base_keys_output = base_left.reshape(row_total, key_feature_width)

    index_list = row_adapter_index.reshape(step_count, row_dev)
    owner_group = index_list // adapter_number
    local_index = index_list % adapter_number
    group_hits = (owner_group[:, :, None] == jnp.arange(groups, dtype=jnp.int32)[None, None, :]).astype(
        jnp.int32
    )
    slot_rank = jnp.sum((jnp.cumsum(group_hits, axis=1) - group_hits) * group_hits, axis=2)
    step_ids = jnp.arange(step_count, dtype=jnp.int32)[:, None]
    slot_index = (owner_group * slots_per_group + step_ids * CAP + slot_rank).reshape(row_total)
    dispatch = (
        slot_index[None, :] == jnp.arange(slot_total, dtype=jnp.int32)[:, None]
    ).astype(jnp.bfloat16)

    tag_values = (local_index + 1).astype(jnp.bfloat16).reshape(row_total, 1)
    tag_block = jnp.broadcast_to(tag_values, (row_total, TAG_WIDTH))
    rows_tagged = jnp.concatenate([gathered_rows, tag_block], axis=1)
    send_rows = jnp.dot(dispatch, rows_tagged, preferred_element_type=jnp.float32).astype(jnp.bfloat16)
    send_rows = send_rows.reshape(groups, slots_per_group, width_per_shard + TAG_WIDTH)
    incoming = lax.all_to_all(send_rows, "ad", split_axis=0, concat_axis=0, tiled=True)
    incoming, base_keys_output = lax.optimization_barrier((incoming, base_keys_output))
    incoming = incoming.reshape(slot_total, width_per_shard + TAG_WIDTH)
    incoming_rows = incoming[:, :width_per_shard]
    incoming_labels = incoming[:, width_per_shard]

    down_all = jnp.einsum(
        "nd,adr->nar", incoming_rows, adapter_down_weight, preferred_element_type=jnp.float32
    )
    labels = (jnp.arange(adapter_number, dtype=jnp.int32) + 1).astype(jnp.bfloat16)
    selector = (incoming_labels[:, None] == labels[None, :]).astype(jnp.float32)
    down_part = jnp.sum(down_all * selector[:, :, None], axis=1)
    shards = lax.axis_size("tp")
    chunk_width = slot_total // shards * rank
    chunks = down_part.reshape(shards, slot_total // shards, rank)
    chunk_sum = jnp.sum(lax.all_to_all(chunks, "tp", split_axis=0, concat_axis=0, tiled=True), axis=0)
    spread = jnp.broadcast_to(chunk_sum[None], (shards,) + chunk_sum.shape)
    down_sum = lax.all_to_all(spread, "tp", split_axis=0, concat_axis=0, tiled=True).reshape(
        slot_total, rank
    )
    down_low = down_sum.astype(jnp.bfloat16)
    spread_rows = (selector.astype(jnp.bfloat16)[:, :, None] * down_low[:, None, :]).reshape(
        slot_total, adapter_number * rank
    )
    up_flat = adapter_up_weight.reshape(adapter_number * rank, key_feature_width)
    adapter_update = jnp.dot(spread_rows, up_flat, preferred_element_type=jnp.float32).astype(
        jnp.bfloat16
    )
    adapter_update = adapter_update.reshape(groups, slots_per_group, key_feature_width)
    rows_sent_back = lax.all_to_all(adapter_update, "ad", split_axis=0, concat_axis=0, tiled=True)
    routed = jnp.dot(
        dispatch.T,
        rows_sent_back.reshape(slot_total, key_feature_width),
        preferred_element_type=jnp.float32,
    )
    out = (base_keys_output + routed).astype(jnp.bfloat16)
    return out.reshape(step_count, row_dev, key_feature_width)


def solution(mesh):
    placed = (
        P(None, "ad", "tp"),
        P(None, "ad"),
        P("tp", None),
        P("ad", "tp", None),
        P("ad", None, "tp"),
    )
    return jax.shard_map(
        body, mesh=mesh, in_specs=placed, out_specs=P(None, "ad", "tp"), check_vma=False
    )
```

```python
import jax
import jax.numpy as jnp
from jax import lax
from jax.sharding import PartitionSpec as P

CAP = 2
TAG_WIDTH = 128


def body(tokens, row_adapter_index, key_base_weight, adapter_down_weight, adapter_up_weight):
    step_count, row_dev, width_per_shard = tokens.shape
    groups = lax.axis_size("ad")
    adapter_number = adapter_down_weight.shape[0]
    rank = adapter_down_weight.shape[2]
    row_total = step_count * row_dev
    slots_per_group = step_count * CAP
    slot_total = groups * slots_per_group

    gathered_rows = tokens.reshape(row_total, width_per_shard)
    partial_base = jnp.dot(gathered_rows, key_base_weight, preferred_element_type=jnp.float32)
    tp_size = lax.axis_size("tp")
    key_feature_width = partial_base.shape[1] // tp_size
    base_pieces = partial_base.reshape(row_total, tp_size, key_feature_width).transpose(1, 0, 2)
    tp_index = lax.axis_index("tp")
    base_left = base_pieces
    bit = 1
    while bit < tp_size:
        base_left = base_left.reshape(base_left.shape[0] // 2, 2, row_total, key_feature_width)
        side = (tp_index // bit) % 2
        keep = lax.dynamic_index_in_dim(base_left, side, axis=1, keepdims=False)
        give = lax.dynamic_index_in_dim(base_left, 1 - side, axis=1, keepdims=False)
        base_left = keep + lax.ppermute(give, "tp", [(k, k ^ bit) for k in range(tp_size)])
        bit *= 2
    base_keys_output = base_left.reshape(row_total, key_feature_width)

    index_list = row_adapter_index.reshape(step_count, row_dev)
    owner_group = index_list // adapter_number
    local_index = index_list % adapter_number
    group_hits = (owner_group[:, :, None] == jnp.arange(groups, dtype=jnp.int32)[None, None, :]).astype(
        jnp.int32
    )
    slot_rank = jnp.sum((jnp.cumsum(group_hits, axis=1) - group_hits) * group_hits, axis=2)
    step_ids = jnp.arange(step_count, dtype=jnp.int32)[:, None]
    slot_index = (owner_group * slots_per_group + step_ids * CAP + slot_rank).reshape(row_total)
    dispatch = (
        slot_index[None, :] == jnp.arange(slot_total, dtype=jnp.int32)[:, None]
    ).astype(jnp.bfloat16)

    tag_values = (local_index + 1).astype(jnp.bfloat16).reshape(row_total, 1)
    tag_block = jnp.broadcast_to(tag_values, (row_total, TAG_WIDTH))
    rows_tagged = jnp.concatenate([gathered_rows, tag_block], axis=1)
    row_of_slot = jnp.sum(
        (slot_index[None, :] == jnp.arange(slot_total, dtype=jnp.int32)[:, None]).astype(jnp.int32)
        * (jnp.arange(row_total, dtype=jnp.int32)[None, :] - row_total),
        axis=1,
    ) + row_total
    rows_padded = jnp.concatenate([rows_tagged, jnp.zeros((1, rows_tagged.shape[1]), rows_tagged.dtype)])
    send_rows = jnp.take(rows_padded, row_of_slot, axis=0, mode="clip")
    send_rows = send_rows.reshape(groups, slots_per_group, width_per_shard + TAG_WIDTH)
    incoming = lax.all_to_all(send_rows, "ad", split_axis=0, concat_axis=0, tiled=True)
    incoming, base_keys_output = lax.optimization_barrier((incoming, base_keys_output))
    incoming = incoming.reshape(slot_total, width_per_shard + TAG_WIDTH)
    incoming_rows = incoming[:, :width_per_shard]
    incoming_labels = incoming[:, width_per_shard]

    down_all = jnp.einsum(
        "nd,adr->nar", incoming_rows, adapter_down_weight, preferred_element_type=jnp.float32
    )
    labels = (jnp.arange(adapter_number, dtype=jnp.int32) + 1).astype(jnp.bfloat16)
    selector = (incoming_labels[:, None] == labels[None, :]).astype(jnp.float32)
    down_part = jnp.sum(down_all * selector[:, :, None], axis=1)
    shards = lax.axis_size("tp")
    chunks = down_part.reshape(shards, slot_total // shards, rank)
    chunk_sum = jnp.sum(lax.all_to_all(chunks, "tp", split_axis=0, concat_axis=0, tiled=True), axis=0)
    spread = jnp.broadcast_to(chunk_sum[None], (shards,) + chunk_sum.shape)
    down_sum = lax.all_to_all(spread, "tp", split_axis=0, concat_axis=0, tiled=True).reshape(
        slot_total, rank
    )
    down_low = down_sum.astype(jnp.bfloat16)
    spread_rows = (selector.astype(jnp.bfloat16)[:, :, None] * down_low[:, None, :]).reshape(
        slot_total, adapter_number * rank
    )
    up_flat = adapter_up_weight.reshape(adapter_number * rank, key_feature_width)
    adapter_update = jnp.dot(spread_rows, up_flat, preferred_element_type=jnp.float32).astype(
        jnp.bfloat16
    )
    adapter_update = adapter_update.reshape(groups, slots_per_group, key_feature_width)
    rows_sent_back = lax.all_to_all(adapter_update, "ad", split_axis=0, concat_axis=0, tiled=True)
    routed = jnp.dot(
        dispatch.T,
        rows_sent_back.reshape(slot_total, key_feature_width),
        preferred_element_type=jnp.float32,
    )
    out = (base_keys_output + routed).astype(jnp.bfloat16)
    return out.reshape(step_count, row_dev, key_feature_width)


def solution(mesh):
    placed = (
        P(None, "ad", "tp"),
        P(None, "ad"),
        P("tp", None),
        P("ad", "tp", None),
        P("ad", None, "tp"),
    )
    return jax.shard_map(
        body, mesh=mesh, in_specs=placed, out_specs=P(None, "ad", "tp"), check_vma=False
    )
```

```python
import jax
import jax.numpy as jnp
from jax import lax
from jax.sharding import PartitionSpec as P

CAP = 2
TAG_WIDTH = 128


def body(tokens, row_adapter_index, key_base_weight, adapter_down_weight, adapter_up_weight):
    step_count, row_dev, width_per_shard = tokens.shape
    groups = lax.axis_size("ad")
    adapter_number = adapter_down_weight.shape[0]
    rank = adapter_down_weight.shape[2]
    row_total = step_count * row_dev
    slots_per_group = step_count * CAP
    slot_total = groups * slots_per_group

    gathered_rows = tokens.reshape(row_total, width_per_shard)
    partial_base = jnp.dot(gathered_rows, key_base_weight, preferred_element_type=jnp.float32)
    tp_size = lax.axis_size("tp")
    key_feature_width = partial_base.shape[1] // tp_size
    base_pieces = partial_base.reshape(row_total, tp_size, key_feature_width).transpose(1, 0, 2)
    tp_index = lax.axis_index("tp")
    base_left = base_pieces
    bit = 1
    while bit < tp_size:
        base_left = base_left.reshape(base_left.shape[0] // 2, 2, row_total, key_feature_width)
        side = (tp_index // bit) % 2
        keep = lax.dynamic_index_in_dim(base_left, side, axis=1, keepdims=False)
        give = lax.dynamic_index_in_dim(base_left, 1 - side, axis=1, keepdims=False)
        base_left = keep + lax.ppermute(give, "tp", [(k, k ^ bit) for k in range(tp_size)])
        bit *= 2
    base_keys_output = base_left.reshape(row_total, key_feature_width)

    index_list = row_adapter_index.reshape(step_count, row_dev)
    owner_group = index_list // adapter_number
    local_index = index_list % adapter_number
    group_hits = (owner_group[:, :, None] == jnp.arange(groups, dtype=jnp.int32)[None, None, :]).astype(
        jnp.int32
    )
    slot_rank = jnp.sum((jnp.cumsum(group_hits, axis=1) - group_hits) * group_hits, axis=2)
    step_ids = jnp.arange(step_count, dtype=jnp.int32)[:, None]
    slot_index = (owner_group * slots_per_group + step_ids * CAP + slot_rank).reshape(row_total)
    dispatch = (
        slot_index[None, :] == jnp.arange(slot_total, dtype=jnp.int32)[:, None]
    ).astype(jnp.bfloat16)

    tag_values = (local_index + 1).astype(jnp.bfloat16).reshape(row_total, 1)
    tag_block = jnp.broadcast_to(tag_values, (row_total, TAG_WIDTH))
    rows_tagged = jnp.concatenate([gathered_rows, tag_block], axis=1)
    send_rows = jnp.dot(dispatch, rows_tagged, preferred_element_type=jnp.float32).astype(jnp.bfloat16)
    send_rows = send_rows.reshape(groups, slots_per_group, width_per_shard + TAG_WIDTH)
    incoming = lax.all_to_all(send_rows, "ad", split_axis=0, concat_axis=0, tiled=True)
    incoming, base_keys_output = lax.optimization_barrier((incoming, base_keys_output))
    incoming = incoming.reshape(slot_total, width_per_shard + TAG_WIDTH)
    incoming_rows = incoming[:, :width_per_shard]
    incoming_labels = incoming[:, width_per_shard]

    down_all = jnp.einsum(
        "nd,adr->nar", incoming_rows, adapter_down_weight, preferred_element_type=jnp.float32
    )
    labels = (jnp.arange(adapter_number, dtype=jnp.int32) + 1).astype(jnp.bfloat16)
    selector = (incoming_labels[:, None] == labels[None, :]).astype(jnp.float32)
    down_part = jnp.sum(down_all * selector[:, :, None], axis=1)
    shards = lax.axis_size("tp")
    copies = jnp.broadcast_to(down_part[None], (shards,) + down_part.shape)
    down_sum = jnp.sum(lax.all_to_all(copies, "tp", split_axis=0, concat_axis=0, tiled=True), axis=0)
    down_low = down_sum.astype(jnp.bfloat16)
    spread_rows = (selector.astype(jnp.bfloat16)[:, :, None] * down_low[:, None, :]).reshape(
        slot_total, adapter_number * rank
    )
    up_flat = adapter_up_weight.reshape(adapter_number * rank, key_feature_width)
    adapter_update = jnp.dot(spread_rows, up_flat, preferred_element_type=jnp.float32).astype(
        jnp.bfloat16
    )
    adapter_update = adapter_update.reshape(groups, slots_per_group, key_feature_width)
    rows_sent_back = lax.all_to_all(adapter_update, "ad", split_axis=0, concat_axis=0, tiled=True)
    routed = jnp.dot(
        dispatch.T,
        rows_sent_back.reshape(slot_total, key_feature_width),
        preferred_element_type=jnp.float32,
    )
    out = (base_keys_output + routed).astype(jnp.bfloat16)
    return out.reshape(step_count, row_dev, key_feature_width)


def solution(mesh):
    placed = (
        P(None, "ad", "tp"),
        P(None, "ad"),
        P("tp", None),
        P("ad", "tp", None),
        P("ad", None, "tp"),
    )
    return jax.shard_map(
        body, mesh=mesh, in_specs=placed, out_specs=P(None, "ad", "tp"), check_vma=False
    )
```

```python
import jax
import jax.numpy as jnp
from jax import lax
from jax.sharding import PartitionSpec as P

CAP = 2
TAG_WIDTH = 128


def body(tokens, row_adapter_index, key_base_weight, adapter_down_weight, adapter_up_weight):
    step_count, row_dev, width_per_shard = tokens.shape
    groups = lax.axis_size("ad")
    adapter_number = adapter_down_weight.shape[0]
    rank = adapter_down_weight.shape[2]
    row_total = step_count * row_dev
    slots_per_group = step_count * CAP
    slot_total = groups * slots_per_group

    gathered_rows = tokens.reshape(row_total, width_per_shard)
    partial_base = jnp.dot(gathered_rows, key_base_weight, preferred_element_type=jnp.float32)
    tp_size = lax.axis_size("tp")
    key_feature_width = partial_base.shape[1] // tp_size
    base_pieces = partial_base.reshape(row_total, tp_size, key_feature_width).transpose(1, 0, 2)
    tp_index = lax.axis_index("tp")
    base_left = base_pieces
    bit = 1
    while bit < tp_size:
        base_left = base_left.reshape(base_left.shape[0] // 2, 2, row_total, key_feature_width)
        side = (tp_index // bit) % 2
        keep = lax.dynamic_index_in_dim(base_left, side, axis=1, keepdims=False)
        give = lax.dynamic_index_in_dim(base_left, 1 - side, axis=1, keepdims=False)
        base_left = keep + lax.ppermute(give, "tp", [(k, k ^ bit) for k in range(tp_size)])
        bit *= 2
    base_keys_output = base_left.reshape(row_total, key_feature_width)

    index_list = row_adapter_index.reshape(step_count, row_dev)
    owner_group = index_list // adapter_number
    local_index = index_list % adapter_number
    group_hits = (owner_group[:, :, None] == jnp.arange(groups, dtype=jnp.int32)[None, None, :]).astype(
        jnp.int32
    )
    slot_rank = jnp.sum((jnp.cumsum(group_hits, axis=1) - group_hits) * group_hits, axis=2)
    step_ids = jnp.arange(step_count, dtype=jnp.int32)[:, None]
    slot_index = (owner_group * slots_per_group + step_ids * CAP + slot_rank).reshape(row_total)
    dispatch = (
        slot_index[None, :] == jnp.arange(slot_total, dtype=jnp.int32)[:, None]
    ).astype(jnp.bfloat16)

    tag_values = (local_index + 1).astype(jnp.bfloat16).reshape(row_total, 1)
    tag_block = jnp.broadcast_to(tag_values, (row_total, TAG_WIDTH))
    rows_tagged = jnp.concatenate([gathered_rows, tag_block], axis=1)
    send_rows = jnp.dot(dispatch, rows_tagged, preferred_element_type=jnp.float32).astype(jnp.bfloat16)
    send_rows = send_rows.reshape(groups, slots_per_group, width_per_shard + TAG_WIDTH)
    incoming = lax.all_to_all(send_rows, "ad", split_axis=0, concat_axis=0, tiled=True)
    incoming, base_keys_output = lax.optimization_barrier((incoming, base_keys_output))
    incoming = incoming.reshape(slot_total, width_per_shard + TAG_WIDTH)
    incoming_rows = incoming[:, :width_per_shard]
    incoming_labels = incoming[:, width_per_shard]

    down_all = jnp.einsum(
        "nd,adr->nar", incoming_rows, adapter_down_weight, preferred_element_type=jnp.float32
    )
    labels = (jnp.arange(adapter_number, dtype=jnp.int32) + 1).astype(jnp.bfloat16)
    selector = (incoming_labels[:, None] == labels[None, :]).astype(jnp.float32)
    down_part = jnp.sum(down_all * selector[:, :, None], axis=1)
    shards = lax.axis_size("tp")
    half_slots = slot_total // 2
    down_halves = down_part.reshape(2, half_slots, rank)
    core = tp_index % 2
    keep_down = lax.dynamic_index_in_dim(down_halves, core, axis=0, keepdims=False)
    give_down = lax.dynamic_index_in_dim(down_halves, 1 - core, axis=0, keepdims=False)
    pair_down = keep_down + lax.ppermute(give_down, "tp", [(k, k ^ 1) for k in range(shards)])
    copies = jnp.broadcast_to(pair_down[None], (shards,) + pair_down.shape)
    moved_down = lax.all_to_all(copies, "tp", split_axis=0, concat_axis=0, tiled=True)
    down_sum = jnp.sum(moved_down.reshape(shards // 2, 2, half_slots, rank), axis=0).reshape(
        slot_total, rank
    )
    down_low = down_sum.astype(jnp.bfloat16)
    spread_rows = (selector.astype(jnp.bfloat16)[:, :, None] * down_low[:, None, :]).reshape(
        slot_total, adapter_number * rank
    )
    up_flat = adapter_up_weight.reshape(adapter_number * rank, key_feature_width)
    adapter_update = jnp.dot(spread_rows, up_flat, preferred_element_type=jnp.float32).astype(
        jnp.bfloat16
    )
    adapter_update = adapter_update.reshape(groups, slots_per_group, key_feature_width)
    rows_sent_back = lax.all_to_all(adapter_update, "ad", split_axis=0, concat_axis=0, tiled=True)
    routed = jnp.dot(
        dispatch.T,
        rows_sent_back.reshape(slot_total, key_feature_width),
        preferred_element_type=jnp.float32,
    )
    out = (base_keys_output + routed).astype(jnp.bfloat16)
    return out.reshape(step_count, row_dev, key_feature_width)


def solution(mesh):
    placed = (
        P(None, "ad", "tp"),
        P(None, "ad"),
        P("tp", None),
        P("ad", "tp", None),
        P("ad", None, "tp"),
    )
    return jax.shard_map(
        body, mesh=mesh, in_specs=placed, out_specs=P(None, "ad", "tp"), check_vma=False
    )
```
